32 devices in a mesh: groups: 2 (over y), blk: 4 (over z), head: 4 (over x, core).
Axes of the slice: x: 2, y: 2, z: 4, core: 2. Of those that a mesh axis runs over, the one named last changes fastest.
Arguments:
- ctx_query: bfloat16 [4096, 8192], P(('groups', 'blk'), 'head'), parts along dimension 0, may hold values from -5 to 5
- ctx_key: bfloat16 [4096, 1024], P(('groups', 'blk'), 'head'), parts along dimension 0, may hold values from -5 to 5
- ctx_value: bfloat16 [4096, 1024], P(('groups', 'blk'), 'head'), parts along dimension 0, may hold values from -4.5 to 4.5
- opt_query: bfloat16 [128, 8192], P(('groups', 'blk'), 'head'), parts along dimension 0, may hold values from -5 to 5
- opt_owner: int32 [128], P('groups'), parts along dimension 0, may hold values from 0 to 3, as said below
- opt_slot: int32 [128], P('groups'), parts along dimension 0, may hold values from 0 to 31, as said below
- opt_length: int32 [128], P('groups'), parts along dimension 0, may hold values from 512 to 2048
Outputs:
- ctx_out: bfloat16 [4096, 8192], P(('groups', 'blk'), 'head'), parts along dimension 0
- opt_out: bfloat16 [256, 8192], P(('groups', 'blk'), 'head'), parts along dimension 0
The draws below stay inside these ranges and needn't reach their ends.
There are 2 independent parts, one for each index of `groups`. The reference program is written for one: setup_inputs(seed, part) draws one part's arguments, and reference() takes and returns one part's arrays. A program takes and returns all parts, laid end to end along the dimension named above; each array names one. Nothing has to cross between parts.
Inputs may be any that keep to these rules, and one draw needn't show every extreme that they name: `opt_owner`: each option token has its own pair of owner block and slot; no block owns more than 32 option tokens, and one block owns exactly 32. `opt_slot`: slots of one owner are distinct.
All inputs are finite; a program needn't handle non-finite values.
Results may differ from the reference program's by a relative error of at most 0.017.
Values may be sent and summed in bfloat16 or wider, within the bound.
A program may use at most 64 MiB of HBM per device.

```python
import jax
import jax.numpy as jnp
from jax import lax

HD = 128
HQ = 64
KVH = 8
BLK = 512
CAP = 32
CTX = 2048
OPTS = 64
N_BLK = 4


def base_values(key, rows, cols):
    return jnp.clip(jax.random.normal(key, (rows, cols), jnp.float32), -4.5, 4.5)


def draw_ctx_key(key, part):
    values = base_values(jax.random.fold_in(key, 11), CTX, KVH * HD)
    return values.astype(jnp.bfloat16)


def draw_ctx_query(key, part):
    values = base_values(jax.random.fold_in(key, 12), CTX, HQ * HD)
    return values.astype(jnp.bfloat16)


def draw_opt_query(key, part):
    values = jax.random.uniform(jax.random.fold_in(key, 13), (OPTS, HQ * HD), jnp.float32, -5.0, 5.0)
    return values.astype(jnp.bfloat16)


def option_places(key):
    base = jax.random.fold_in(key, 21)
    slot_count = N_BLK * CAP
    full_owner = jax.random.randint(jax.random.fold_in(base, 1), (), 0, N_BLK)
    owner_bias = jax.random.randint(jax.random.fold_in(base, 2), (N_BLK,), 0, 3)
    noise = jax.random.randint(jax.random.fold_in(base, 3), (slot_count,), 0, 65536)
    slot_ids = jnp.arange(slot_count, dtype=jnp.int32)
    owners = slot_ids // CAP
    score = noise + owner_bias[owners] * 32768 + (owners == full_owner).astype(jnp.int32) * 262144
    ranked = jnp.argsort(-(score * slot_count + slot_ids))
    chosen = ranked[:OPTS].astype(jnp.int32)
    shuffle = jax.random.permutation(jax.random.fold_in(base, 4), OPTS)
    chosen = chosen[shuffle]
    return ((chosen // CAP).astype(jnp.int32), (chosen % CAP).astype(jnp.int32))


def draw_opt_owner(key, part):
    return option_places(key)[0]


def draw_opt_slot(key, part):
    return option_places(key)[1]


def place_ends(drawn, own_key, low, high):
    place = [jax.random.randint(jax.random.fold_in(own_key, axis), (), 0, length) for axis, length in enumerate(drawn.shape)]
    main_axis = drawn.shape.index(max(drawn.shape))
    beside = place[:main_axis] + [(place[main_axis] + 1) % drawn.shape[main_axis]] + place[main_axis + 1:]
    return drawn.at[tuple(place)].set(low).at[tuple(beside)].set(high)


def levels(stream_key, shape, pieces, low, high):
    level, own = 1.0, jax.random.fold_in(stream_key, 6)
    for axis_at, blocks in pieces:
        draws = jnp.exp(jax.random.uniform(jax.random.fold_in(own, axis_at), (blocks,), jnp.float32, low / len(pieces), high / len(pieces)))
        level = level * jnp.repeat(draws, shape[axis_at] // blocks).reshape([-1 if axis == axis_at else 1 for axis in range(len(shape))])
    return level


def normal_values(rng, extent, deviation, limit, split=(), held_as=jnp.bfloat16):
    values = deviation * jax.random.normal(rng, extent, jnp.float32)
    if split:
        values = values * levels(rng, extent, split, -0.22, 0.18)
    return jnp.clip(values, -limit, limit).astype(held_as)


def setup_inputs(seed: int = 0, part: int = 0) -> dict:
    key_list = jax.random.split(jax.random.key(seed), 8)
    own_keys = jax.random.split(jax.random.fold_in(key_list[7], part), 8)
    return {
        "ctx_query": draw_ctx_query(jax.random.fold_in(jax.random.fold_in(key_list[7], part), 71), part),
        "ctx_key": draw_ctx_key(jax.random.fold_in(jax.random.fold_in(key_list[7], part), 71), part),
        "ctx_value": normal_values(own_keys[2], (CTX, KVH * HD), 1.0, 4.5, ((0, 4), (1, 4))),
        "opt_query": draw_opt_query(jax.random.fold_in(jax.random.fold_in(key_list[7], part), 71), part),
        "opt_owner": draw_opt_owner(jax.random.fold_in(jax.random.fold_in(key_list[7], part), 71), part),
        "opt_slot": draw_opt_slot(jax.random.fold_in(jax.random.fold_in(key_list[7], part), 71), part),
        "opt_length": place_ends(jax.random.randint(own_keys[6], (OPTS,), BLK, CTX + 1), jax.random.fold_in(own_keys[6], 1), BLK, CTX).astype(jnp.int32),
    }


def reference(ctx_query, ctx_key, ctx_value, opt_query, opt_owner, opt_slot, opt_length):
    group_size = HQ // KVH
    scale = HD ** -0.5
    high = lax.Precision.HIGHEST
    query_all = ctx_query.reshape(N_BLK, BLK, HQ, HD)
    key_all = ctx_key.reshape(N_BLK, BLK, KVH, HD)
    value_all = ctx_value.reshape(N_BLK, BLK, KVH, HD)
    anchor_key = jnp.repeat(key_all[0], group_size, axis=1).astype(jnp.float32)
    anchor_value = jnp.repeat(value_all[0], group_size, axis=1).astype(jnp.float32)
    spots = jnp.arange(BLK, dtype=jnp.int32)
    causal = spots[:, None] >= spots[None, :]

    def first_phase(index):
        query_blk = query_all[index].astype(jnp.float32)
        key_blk = jnp.repeat(key_all[index], group_size, axis=1).astype(jnp.float32)
        value_blk = jnp.repeat(value_all[index], group_size, axis=1).astype(jnp.float32)
        local = jnp.einsum('thd,shd->hts', query_blk, key_blk, precision=high) * scale
        local = jnp.where(causal[None], local, -1e30)
        remote = jnp.einsum('thd,shd->hts', query_blk, anchor_key, precision=high) * scale
        remote = jnp.where(index > 0, remote, -1e30)
        top = jnp.maximum(jnp.max(local, axis=2), jnp.max(remote, axis=2))
        e_local = jnp.exp(local - top[..., None])
        e_remote = jnp.exp(remote - top[..., None])
        total = jnp.sum(e_local, axis=2) + jnp.sum(e_remote, axis=2)
        acc = jnp.einsum('hts,shd->thd', e_local.astype(jnp.bfloat16).astype(jnp.float32), value_blk, precision=high)
        acc = acc + jnp.einsum('hts,shd->thd', e_remote.astype(jnp.bfloat16).astype(jnp.float32), anchor_value, precision=high)
        return (acc / total.T[:, :, None]).astype(jnp.bfloat16)

    ctx_out = lax.map(first_phase, jnp.arange(N_BLK, dtype=jnp.int32)).reshape(CTX, HQ * HD)

    option_q = opt_query.reshape(OPTS, HQ, HD).astype(jnp.float32)

    def second_phase(index):
        key_blk = jnp.repeat(key_all[index], group_size, axis=1).astype(jnp.float32)
        value_blk = jnp.repeat(value_all[index], group_size, axis=1).astype(jnp.float32)
        scores = jnp.einsum('ihd,shd->his', option_q, key_blk, precision=high) * scale
        count = jnp.clip(opt_length - index * BLK, 0, BLK)
        visible = spots[None, :] < count[:, None]
        scores = jnp.where(visible[None], scores, -1e30)
        top = jnp.max(scores, axis=2)
        expo = jnp.exp(scores - top[..., None])
        total = jnp.sum(expo, axis=2)
        acc = jnp.einsum('his,shd->ihd', expo.astype(jnp.bfloat16).astype(jnp.float32), value_blk, precision=high)
        live = count > 0
        part = jnp.where(live[:, None, None], acc / total.T[:, :, None], 0.0).astype(jnp.bfloat16)
        stat = jnp.where(live[:, None], (top + jnp.log(total)).T, -1e30)
        return part, stat

    parts, stats = lax.map(second_phase, jnp.arange(N_BLK, dtype=jnp.int32))
    top_all = jnp.max(stats, axis=0)
    weight = jnp.exp(stats - top_all[None])
    merged = jnp.sum(weight[..., None] * parts.astype(jnp.float32), axis=0) / jnp.sum(weight, axis=0)[..., None]
    where_to = (opt_owner * CAP + opt_slot).astype(jnp.int32)
    opt_out = jnp.zeros((CAP * N_BLK, HQ * HD), jnp.bfloat16).at[where_to].set(merged.reshape(OPTS, HQ * HD).astype(jnp.bfloat16))
    return ctx_out, opt_out
```

```python
import functools
import math

import jax
import jax.numpy as jnp
from jax import lax
from jax.experimental import pallas as pl
from jax.experimental.pallas import tpu as pltpu
from jax.sharding import PartitionSpec as P

HD = 128
HQ = 64
KVH = 8
CAP = 32
GROUP = HQ // KVH
MESH = pl.DeviceIdType.MESH
NEG = -1e30
LN2 = math.log(2.0)
COEF = HD**-0.5 / LN2
QUARTERS = 4
PAIR = 2


def dot_nt(a, b):
    return lax.dot_general(a, b, (((1,), (1,)), ((), ())), preferred_element_type=jnp.float32)


def dot_nn(a, b, precision=None):
    return lax.dot_general(
        a, b, (((1,), (0,)), ((), ())), preferred_element_type=jnp.float32, precision=precision
    )


def kernel(
    n,
    q_hbm, k_hbm, v_hbm, oq_hbm, len_ref, dest_ref,
    ctx_hbm, opt_ref,
    q_ref, k_ref, vx_ref, ak_ref, avx_ref, oq_ref, acc_ref, m_ref, out_ref,
    part_ref, stat_ref, pbuf, sbuf, rx_p, rx_s,
    q_sem, k_sem, v_sem, o_sem, out_sem,
    oq_send, oq_recv, ak_send, ak_recv, av_send, av_recv,
    p_send, p_recv, s_send, s_recv,
):
    me = lax.axis_index("blk")
    rows = q_ref.shape[0]
    heads = q_ref.shape[1] // HD
    kvs = k_ref.shape[1] // HD
    entry = oq_hbm.shape[0]
    opts = oq_ref.shape[0]
    chunk = rows // QUARTERS
    pairs = heads // PAIR
    per_group = GROUP // PAIR
    tile = rows // 2
    half = heads // 2 * HD

    q_copies = [
        pltpu.make_async_copy(
            q_hbm.at[:, pl.ds(s * half, half)], q_ref.at[:, pl.ds(s * half, half)], q_sem.at[s]
        )
        for s in range(2)
    ]
    k_copy = pltpu.make_async_copy(k_hbm, k_ref, k_sem)
    ones = jnp.ones((rows, HD), jnp.bfloat16)
    for g in range(kvs):
        vx_ref[g, :, HD:] = ones
        avx_ref[g, :, HD:] = ones
    v_copies = [
        pltpu.make_async_copy(
            v_hbm.at[:, pl.ds(g * HD, HD)], vx_ref.at[g, :, pl.ds(0, HD)], v_sem.at[g]
        )
        for g in range(kvs)
    ]
    own = pl.ds(pl.multiple_of(me * entry, entry), entry)
    o_copy = pltpu.make_async_copy(oq_hbm, oq_ref.at[own], o_sem)
    k_copy.start()
    for copy in v_copies:
        copy.start()
    q_copies[0].start()
    q_copies[1].start()
    o_copy.start()

    barrier = pltpu.get_barrier_semaphore()
    for step in range(1, n):
        pl.semaphore_signal(
            barrier, inc=1, device_id={"blk": lax.rem(me + step, n)}, device_id_type=MESH
        )
    pl.semaphore_wait(barrier, n - 1)

    def oq_copy(step):
        return pltpu.make_async_remote_copy(
            src_ref=oq_hbm,
            dst_ref=oq_ref.at[own],
            send_sem=oq_send.at[step - 1],
            recv_sem=oq_recv.at[step - 1],
            device_id={"blk": lax.rem(me + step, n)},
            device_id_type=MESH,
        )

    for step in range(1, n):
        oq_copy(step).start()

    k_copy.wait()
    for copy in v_copies:
        copy.wait()

    up = lax.rem(me + 1, n)

    def anchor_copies(c, from_own):
        g = c // QUARTERS
        r = lax.rem(c, QUARTERS)
        span = pl.ds(pl.multiple_of(r * chunk, chunk), chunk)
        cols = pl.ds(pl.multiple_of(g * HD, HD), HD)
        key_from = k_ref if from_own else ak_ref
        value_from = vx_ref if from_own else avx_ref
        return (
            pltpu.make_async_remote_copy(
                src_ref=key_from.at[span, cols],
                dst_ref=ak_ref.at[span, cols],
                send_sem=ak_send.at[c],
                recv_sem=ak_recv.at[c],
                device_id={"blk": up},
                device_id_type=MESH,
            ),
            pltpu.make_async_remote_copy(
                src_ref=value_from.at[g, span, pl.ds(0, HD)],
                dst_ref=avx_ref.at[g, span, pl.ds(0, HD)],
                send_sem=av_send.at[c],
                recv_sem=av_recv.at[c],
                device_id={"blk": up},
                device_id_type=MESH,
            ),
        )

    chunks = QUARTERS * kvs

    @pl.when(me == 0)
    def _():
        def send(c, carry):
            for copy in anchor_copies(c, True):
                copy.start()
            return carry

        lax.fori_loop(0, chunks, send, 0)

    def forward(c):
        @pl.when(me > 0)
        def _():
            for copy in anchor_copies(c, False):
                copy.wait_recv()

            @pl.when(me < n - 1)
            def _():
                for copy in anchor_copies(c, False):
                    copy.start()

    def head_cols(h):
        return pl.ds(pl.multiple_of(h * HD, HD), HD)

    diag_row = lax.broadcasted_iota(jnp.int32, (tile, tile), 0)
    diag_col = lax.broadcasted_iota(jnp.int32, (tile, tile), 1)
    causal = diag_row >= diag_col

    def local_head(h):
        g = h // GROUP
        for t in range(2):
            span = pl.ds(t * tile, tile)
            query = q_ref[span, head_cols(h)]
            diag = dot_nt(query, k_ref[span, head_cols(g)])
            diag = jnp.where(causal, diag, NEG)
            top = jnp.max(diag, axis=1, keepdims=True)
            if t:
                rest = dot_nt(query, k_ref[pl.ds(0, t * tile), head_cols(g)])
                top = jnp.maximum(top, jnp.max(rest, axis=1, keepdims=True))
            top = top * COEF
            acc = dot_nn(jnp.exp2(diag * COEF - top).astype(jnp.bfloat16), vx_ref[g, span, :])
            if t:
                acc = acc + dot_nn(
                    jnp.exp2(rest * COEF - top).astype(jnp.bfloat16),
                    vx_ref[g, pl.ds(0, t * tile), :],
                )
            acc_ref[h, span, :] = acc
            m_ref[h, span, :] = jnp.broadcast_to(top, (tile, HD))

    def anchor_head(h):
        g = h // GROUP
        for t in range(2):
            span = pl.ds(t * tile, tile)
            query = q_ref[span, head_cols(h)]
            score = dot_nt(query, ak_ref[:, head_cols(g)])
            before = m_ref[h, span, :]
            top = jnp.maximum(jnp.max(score, axis=1, keepdims=True) * COEF, before[:, :1])
            acc = dot_nn(jnp.exp2(score * COEF - top).astype(jnp.bfloat16), avx_ref[g])
            alpha = jnp.exp2(before - top)
            value = acc[:, :HD] + alpha * acc_ref[h, span, pl.ds(0, HD)]
            total = acc[:, HD:] + alpha * acc_ref[h, span, pl.ds(HD, HD)]
            out_ref[span, head_cols(h)] = (value / total).astype(jnp.bfloat16)

    offset = pairs - QUARTERS

    def local_pair(i, carry):
        for j in range(PAIR):
            local_head(i * PAIR + j)

        @pl.when(i >= offset)
        def _():
            forward(i - offset)

        return carry

    dest = dest_ref[...]
    length = len_ref[...].astype(jnp.float32)

    def opt_attend(queries, count, key, value_x):
        size = queries.shape[0]
        stacked = jnp.concatenate([queries[:, j * HD : (j + 1) * HD] for j in range(GROUP)], axis=0)
        counts = jnp.concatenate([count] * GROUP, axis=0)
        score = dot_nt(stacked, key)
        spot = lax.broadcasted_iota(jnp.int32, score.shape, 1).astype(jnp.float32)
        score = jnp.where(spot < counts, score, NEG)
        top = jnp.max(score, axis=1, keepdims=True) * COEF
        acc = dot_nn(jnp.exp2(score * COEF - top).astype(jnp.bfloat16), value_x)
        total = acc[:, HD:]
        live = counts > 0.0
        part = jnp.where(live, acc[:, :HD] / total, 0.0).astype(jnp.bfloat16)
        stat = jnp.where(live, top * LN2 + jnp.log(total), NEG)
        return (
            [part[j * size : (j + 1) * size] for j in range(GROUP)],
            [stat[j * size : (j + 1) * size] for j in range(GROUP)],
        )

    step_rows = min(opts, 64)

    def options_blk():
        for base in range(0, opts, step_rows):
            span = pl.ds(base, step_rows)
            eye = lax.broadcasted_iota(jnp.int32, (step_rows, opts), 0) + base
            eye = eye == lax.broadcasted_iota(jnp.int32, (step_rows, opts), 1)
            col = jnp.sum(jnp.where(eye, length, 0.0), axis=1, keepdims=True)
            start = (me * rows).astype(jnp.float32)
            count = jnp.clip(col - start, 0.0, float(rows))
            lanes = lax.broadcasted_iota(jnp.int32, (step_rows, HD), 1)
            stats = jnp.zeros((step_rows, HD), jnp.float32)
            for g in range(kvs):
                queries = oq_ref[span, pl.ds(g * GROUP * HD, GROUP * HD)]
                parts, tops = opt_attend(queries, count, k_ref[:, pl.ds(g * HD, HD)], vx_ref[g])
                for j in range(GROUP):
                    h = g * GROUP + j
                    part_ref[span, pl.ds(h * HD, HD)] = parts[j]
                    stats = jnp.where(lanes == h, tops[j], stats)
            stat_ref[span, :] = stats
        slots = lax.broadcasted_iota(jnp.int32, (CAP, opts), 0)
        for d in range(n):
            hot = (slots + d * CAP == dest).astype(jnp.float32)
            span = pl.ds(d * CAP, CAP)
            pbuf[span, :] = dot_nn(hot.astype(jnp.bfloat16), part_ref[...]).astype(jnp.bfloat16)
            sbuf[span, :] = dot_nn(hot, stat_ref[...], lax.Precision.HIGHEST)

    def part_copies(step):
        to = lax.rem(me + step, n)
        span = pl.ds(pl.multiple_of(to * CAP, CAP), CAP)
        return (
            pltpu.make_async_remote_copy(
                src_ref=pbuf.at[span],
                dst_ref=rx_p.at[me],
                send_sem=p_send.at[step - 1],
                recv_sem=p_recv.at[step - 1],
                device_id={"blk": to},
                device_id_type=MESH,
            ),
            pltpu.make_async_remote_copy(
                src_ref=sbuf.at[span],
                dst_ref=rx_s.at[me],
                send_sem=s_send.at[step - 1],
                recv_sem=s_recv.at[step - 1],
                device_id={"blk": to},
                device_id_type=MESH,
            ),
        )

    mine_hot = (lax.broadcasted_iota(jnp.int32, (CAP, opts), 0) + me * CAP) == dest

    def options_anchor(key_of, value_of):
        count = jnp.sum(jnp.where(mine_hot, length, 0.0), axis=1, keepdims=True)
        count = jnp.clip(count, 0.0, float(rows))
        hot = mine_hot.astype(jnp.float32).astype(jnp.bfloat16)
        lanes = lax.broadcasted_iota(jnp.int32, (CAP, HD), 1)
        stats = jnp.zeros((CAP, HD), jnp.float32)
        for g in range(kvs):
            cols = pl.ds(g * GROUP * HD, GROUP * HD)
            queries = dot_nn(hot, oq_ref[:, cols]).astype(jnp.bfloat16)
            parts, tops = opt_attend(queries, count, key_of[:, pl.ds(g * HD, HD)], value_of[g])
            for j in range(GROUP):
                h = g * GROUP + j
                rx_p[0, :, pl.ds(h * HD, HD)] = parts[j]
                stats = jnp.where(lanes == h, tops[j], stats)
        rx_s[0] = stats

    cut = pairs // 2
    for copy in q_copies:
        copy.wait()
    lax.fori_loop(0, cut, local_pair, 0)
    o_copy.wait()
    for step in range(1, n):
        oq_copy(step).wait()

    @pl.when(me > 0)
    def _():
        options_blk()

    lax.fori_loop(cut, pairs, local_pair, 0)

    @pl.when(me > 0)
    def _():
        for step in range(1, n):
            for copy in part_copies(step):
                copy.start()
        own_slots = pl.ds(pl.multiple_of(me * CAP, CAP), CAP)
        rx_p[me] = pbuf[own_slots, :]
        rx_s[me] = sbuf[own_slots, :]

    def out_copy(i):
        cols = pl.ds(pl.multiple_of(i * PAIR * HD, PAIR * HD), PAIR * HD)
        return pltpu.make_async_copy(out_ref.at[:, cols], ctx_hbm.at[:, cols], out_sem.at[i])

    @pl.when(me == 0)
    def _():
        def finish(i, carry):
            for j in range(PAIR):
                h = i * PAIR + j
                out_ref[:, head_cols(h)] = (
                    acc_ref[h, :, pl.ds(0, HD)] / acc_ref[h, :, pl.ds(HD, HD)]
                ).astype(jnp.bfloat16)
            out_copy(i).start()
            return carry

        lax.fori_loop(0, pairs, finish, 0)
        options_anchor(k_ref, vx_ref)

    @pl.when(me > 0)
    def _():
        def finish(i, carry):
            for j in range(PAIR):
                anchor_head(i * PAIR + j)
            out_copy(i).start()

            @pl.when(i + QUARTERS < chunks)
            def _():
                forward(i + QUARTERS)

            return carry

        lax.fori_loop(0, pairs, finish, 0)
        options_anchor(ak_ref, avx_ref)

    for step in range(1, n):
        @pl.when(lax.rem(me - step + n, n) > 0)
        def _():
            for copy in part_copies(step):
                copy.wait_recv()

    top = rx_s[0]
    for b in range(1, n):
        top = jnp.maximum(top, rx_s[b])
    total = jnp.zeros_like(top)
    for b in range(n):
        total = total + jnp.exp(rx_s[b] - top)
    occupied = jnp.sum(mine_hot.astype(jnp.float32), axis=1, keepdims=True) > 0.0
    for h in range(heads):
        cols = pl.ds(h * HD, HD)
        merged = jnp.zeros((CAP, HD), jnp.float32)
        for b in range(n):
            weight = jnp.exp(rx_s[b, :, pl.ds(h, 1)] - top[:, h : h + 1])
            merged = merged + weight * rx_p[b, :, cols].astype(jnp.float32)
        merged = merged / total[:, h : h + 1]
        opt_ref[:, cols] = jnp.where(occupied, merged, 0.0).astype(jnp.bfloat16)

    @pl.when(me == 0)
    def _():
        def drain(c, carry):
            for copy in anchor_copies(c, True):
                copy.wait_send()
            return carry

        lax.fori_loop(0, chunks, drain, 0)

    @pl.when((me > 0) & (me < n - 1))
    def _():
        def drain(c, carry):
            for copy in anchor_copies(c, False):
                copy.wait_send()
            return carry

        lax.fori_loop(0, chunks, drain, 0)

    @pl.when(me > 0)
    def _():
        for step in range(1, n):
            for copy in part_copies(step):
                copy.wait_send()

    def drain_out(i, carry):
        out_copy(i).wait()
        return carry

    lax.fori_loop(0, pairs, drain_out, 0)


def body(ctx_query, ctx_key, ctx_value, opt_query, opt_owner, opt_slot, opt_length):
    n = lax.axis_size("blk")
    rows, width = ctx_query.shape
    heads = width // HD
    kvs = ctx_key.shape[1] // HD
    opts = opt_length.shape[0]
    entry = opt_query.shape[0]
    chunks = QUARTERS * kvs
    dest = (opt_owner * CAP + opt_slot).reshape(1, opts)
    bf16, f32 = jnp.bfloat16, jnp.float32
    dma = pltpu.SemaphoreType.DMA
    hbm = pl.BlockSpec(memory_space=pl.ANY)
    vmem = pl.BlockSpec(memory_space=pltpu.VMEM)
    return pl.pallas_call(
        functools.partial(kernel, n),
        out_shape=(
            jax.ShapeDtypeStruct((rows, width), bf16),
            jax.ShapeDtypeStruct((CAP, width), bf16),
        ),
        in_specs=[hbm, hbm, hbm, hbm, vmem, vmem],
        out_specs=(hbm, vmem),
        scratch_shapes=[
            pltpu.VMEM((rows, width), bf16),
            pltpu.VMEM((rows, kvs * HD), bf16),
            pltpu.VMEM((kvs, rows, 2 * HD), bf16),
            pltpu.VMEM((rows, kvs * HD), bf16),
            pltpu.VMEM((kvs, rows, 2 * HD), bf16),
            pltpu.VMEM((opts, width), bf16),
            pltpu.VMEM((heads, rows, 2 * HD), f32),
            pltpu.VMEM((heads, rows, HD), f32),
            pltpu.VMEM((rows, width), bf16),
            pltpu.VMEM((opts, width), bf16),
            pltpu.VMEM((opts, HD), f32),
            pltpu.VMEM((n * CAP, width), bf16),
            pltpu.VMEM((n * CAP, HD), f32),
            pltpu.VMEM((n, CAP, width), bf16),
            pltpu.VMEM((n, CAP, HD), f32),
            dma((2,)), dma(()), dma((kvs,)), dma(()), dma((heads // PAIR,)),
            dma((n - 1,)), dma((n - 1,)),
            dma((chunks,)), dma((chunks,)), dma((chunks,)), dma((chunks,)),
            dma((n - 1,)), dma((n - 1,)), dma((n - 1,)), dma((n - 1,)),
        ],
        compiler_params=pltpu.CompilerParams(
            collective_id=0, has_side_effects=True, vmem_limit_bytes=60 * 1024 * 1024
        ),
        name="star",
    )(ctx_query, ctx_key, ctx_value, opt_query, opt_length.reshape(1, opts), dest)


def solution(mesh):
    return jax.shard_map(
        body,
        mesh=mesh,
        in_specs=(
            P(("groups", "blk"), "head"),
            P(("groups", "blk"), "head"),
            P(("groups", "blk"), "head"),
            P(("groups", "blk"), "head"),
            P("groups"),
            P("groups"),
            P("groups"),
        ),
        out_specs=(P(("groups", "blk"), "head"), P(("groups", "blk"), "head")),
        check_vma=False,
    )
```

```python
import functools
import math

import jax
import jax.numpy as jnp
from jax import lax
from jax.experimental import pallas as pl
from jax.experimental.pallas import tpu as pltpu
from jax.sharding import PartitionSpec as P

HD = 128
HQ = 64
KVH = 8
CAP = 32
GROUP = HQ // KVH
MESH = pl.DeviceIdType.MESH
NEG = -1e30
LN2 = math.log(2.0)
COEF = HD**-0.5 / LN2
QUARTERS = 4
PAIR = 2


def dot_nt(a, b):
    return lax.dot_general(a, b, (((1,), (1,)), ((), ())), preferred_element_type=jnp.float32)


def dot_nn(a, b, precision=None):
    return lax.dot_general(
        a, b, (((1,), (0,)), ((), ())), preferred_element_type=jnp.float32, precision=precision
    )


def kernel(
    n,
    q_hbm, k_hbm, v_hbm, oq_hbm, len_ref, owner_ref, slot_ref,
    ctx_hbm, opt_ref,
    q_ref, k_ref, vx_ref, ak_ref, avx_ref, oq_ref, acc_ref, m_ref, out_ref,
    part_ref, stat_ref, pbuf, sbuf, rx_p, rx_s,
    q_sem, k_sem, v_sem, o_sem, out_sem,
    oq_send, oq_recv, ou_send, ou_recv, ak_send, ak_recv, av_send, av_recv,
    p_send, p_recv, s_send, s_recv,
):
    me = lax.axis_index("blk")
    rows = q_ref.shape[0]
    heads = q_ref.shape[1] // HD
    kvs = k_ref.shape[1] // HD
    entry = oq_hbm.shape[0]
    opts = oq_ref.shape[0]
    chunk = rows // QUARTERS
    pairs = heads // PAIR
    per_group = GROUP // PAIR
    tile = rows // 2
    half = heads // 2 * HD

    q_copies = [
        pltpu.make_async_copy(
            q_hbm.at[:, pl.ds(s * half, half)], q_ref.at[:, pl.ds(s * half, half)], q_sem.at[s]
        )
        for s in range(2)
    ]
    k_copy = pltpu.make_async_copy(k_hbm, k_ref, k_sem)
    ones = jnp.ones((rows, HD), jnp.bfloat16)
    for g in range(kvs):
        vx_ref[g, :, HD:] = ones
        avx_ref[g, :, HD:] = ones
    v_copies = [
        pltpu.make_async_copy(
            v_hbm.at[:, pl.ds(g * HD, HD)], vx_ref.at[g, :, pl.ds(0, HD)], v_sem.at[g]
        )
        for g in range(kvs)
    ]
    own = pl.ds(pl.multiple_of(me * entry, entry), entry)
    o_copy = pltpu.make_async_copy(oq_hbm, oq_ref.at[own], o_sem)
    k_copy.start()
    for copy in v_copies:
        copy.start()
    q_copies[0].start()
    q_copies[1].start()
    o_copy.start()

    barrier = pltpu.get_barrier_semaphore()
    for step in range(1, n):
        pl.semaphore_signal(
            barrier, inc=1, device_id={"blk": lax.rem(me + step, n)}, device_id_type=MESH
        )
    pl.semaphore_wait(barrier, n - 1)

    def oq_down(step):
        return pltpu.make_async_remote_copy(
            src_ref=oq_hbm,
            dst_ref=oq_ref.at[own],
            send_sem=oq_send.at[step - 1],
            recv_sem=oq_recv.at[step - 1],
            device_id={"blk": lax.rem(me - step + n, n)},
            device_id_type=MESH,
        )

    def oq_up(step):
        at = lax.rem(me - step + 1 + n, n)
        span = pl.ds(pl.multiple_of(at * entry, entry), entry)
        return pltpu.make_async_remote_copy(
            src_ref=oq_hbm if step == 1 else oq_ref.at[span],
            dst_ref=oq_ref.at[span],
            send_sem=ou_send.at[step - 1],
            recv_sem=ou_recv.at[step - 1],
            device_id={"blk": lax.rem(me + 1, n)},
            device_id_type=MESH,
        )

    def oq_up_arrived(step):
        @pl.when(me >= step)
        def _():
            oq_up(step).wait_recv()

    def oq_up_start(step):
        @pl.when((me >= step - 1) & (me < n - 1))
        def _():
            oq_up(step).start()

    oq_up_start(1)
    for step in range(1, n):
        @pl.when(me >= step)
        def _():
            oq_down(step).start()

    k_copy.wait()
    for copy in v_copies:
        copy.wait()

    up = lax.rem(me + 1, n)

    def anchor_copies(c, from_own):
        g = c // QUARTERS
        r = lax.rem(c, QUARTERS)
        span = pl.ds(pl.multiple_of(r * chunk, chunk), chunk)
        cols = pl.ds(pl.multiple_of(g * HD, HD), HD)
        key_from = k_ref if from_own else ak_ref
        value_from = vx_ref if from_own else avx_ref
        return (
            pltpu.make_async_remote_copy(
                src_ref=key_from.at[span, cols],
                dst_ref=ak_ref.at[span, cols],
                send_sem=ak_send.at[c],
                recv_sem=ak_recv.at[c],
                device_id={"blk": up},
                device_id_type=MESH,
            ),
            pltpu.make_async_remote_copy(
                src_ref=value_from.at[g, span, pl.ds(0, HD)],
                dst_ref=avx_ref.at[g, span, pl.ds(0, HD)],
                send_sem=av_send.at[c],
                recv_sem=av_recv.at[c],
                device_id={"blk": up},
                device_id_type=MESH,
            ),
        )

    chunks = QUARTERS * kvs

    @pl.when(me == 0)
    def _():
        def send(c, carry):
            for copy in anchor_copies(c, True):
                copy.start()
            return carry

        lax.fori_loop(0, chunks, send, 0)

    def forward(c):
        @pl.when(me > 0)
        def _():
            for copy in anchor_copies(c, False):
                copy.wait_recv()

            @pl.when(me < n - 1)
            def _():
                for copy in anchor_copies(c, False):
                    copy.start()

    def head_cols(h):
        return pl.ds(pl.multiple_of(h * HD, HD), HD)

    diag_row = lax.broadcasted_iota(jnp.int32, (tile, tile), 0)
    diag_col = lax.broadcasted_iota(jnp.int32, (tile, tile), 1)
    causal = diag_row >= diag_col

    def local_heads(hs):
        units = [(h, t) for h in hs for t in range(2)]
        raw, tops, probs = {}, {}, {}

        def scores(u):
            h, t = units[u]
            g = h // GROUP
            query = q_ref[pl.ds(t * tile, tile), head_cols(h)]
            parts = [dot_nt(query, k_ref[pl.ds(j * tile, tile), head_cols(g)]) for j in range(t + 1)]
            parts[t] = jnp.where(causal, parts[t], NEG)
            top = functools.reduce(jnp.maximum, parts)
            tops[u] = jnp.max(top, axis=1, keepdims=True) * COEF
            raw[u] = parts

        def soften(u):
            probs[u] = [jnp.exp2(x * COEF - tops[u]).astype(jnp.bfloat16) for x in raw.pop(u)]

        def gather(u):
            h, t = units[u]
            g = h // GROUP
            span = pl.ds(t * tile, tile)
            prob = jnp.concatenate(probs.pop(u), axis=1)
            acc_ref[h, span, :] = dot_nn(prob, vx_ref[g, pl.ds(0, (t + 1) * tile), :])
            m_ref[h, span, :] = jnp.broadcast_to(tops[u], (tile, HD))

        staged(units, scores, soften, gather)

    def staged(units, scores, soften, gather):
        count = len(units)
        for k in range(count + 2):
            if k < count:
                scores(k)
            if 0 <= k - 1 < count:
                soften(k - 1)
            if 0 <= k - 2 < count:
                gather(k - 2)

    def anchor_heads(hs):
        units = [(h, t) for h in hs for t in range(2)]
        raw, tops, probs = {}, {}, {}

        def scores(u):
            h, t = units[u]
            span = pl.ds(t * tile, tile)
            raw[u] = dot_nt(q_ref[span, head_cols(h)], ak_ref[:, head_cols(h // GROUP)])
            top = jnp.max(raw[u], axis=1, keepdims=True) * COEF
            tops[u] = jnp.maximum(top, m_ref[h, span, :][:, :1])

        def soften(u):
            probs[u] = jnp.exp2(raw.pop(u) * COEF - tops[u]).astype(jnp.bfloat16)

        def gather(u):
            h, t = units[u]
            span = pl.ds(t * tile, tile)
            acc = dot_nn(probs.pop(u), avx_ref[h // GROUP])
            alpha = jnp.exp2(m_ref[h, span, :] - tops[u])
            value = acc[:, :HD] + alpha * acc_ref[h, span, pl.ds(0, HD)]
            total = acc[:, HD:] + alpha * acc_ref[h, span, pl.ds(HD, HD)]
            out_ref[span, head_cols(h)] = (value / total).astype(jnp.bfloat16)

        staged(units, scores, soften, gather)

    cut = pairs - 1
    offset = max(pairs - QUARTERS - 1, 0) + 2 * (me - 1)

    def local_pair(i, carry):
        local_heads([i * PAIR + j for j in range(PAIR)])

        for step in range(1, n - 1):
            @pl.when(i == min(2 * step, cut - 1))
            def _():
                oq_up_arrived(step)
                oq_up_start(step + 1)

        @pl.when((me > 0) & (i >= offset) & (i < offset + chunks))
        def _():
            forward(i - offset)

        return carry

    dest = owner_ref[...] * CAP + slot_ref[...]
    length = len_ref[...].astype(jnp.float32)

    def opt_attend(queries, count, key, value_x):
        size = queries.shape[0]
        stacked = jnp.concatenate([queries[:, j * HD : (j + 1) * HD] for j in range(GROUP)], axis=0)
        counts = jnp.concatenate([count] * GROUP, axis=0)
        score = dot_nt(stacked, key)
        spot = lax.broadcasted_iota(jnp.int32, score.shape, 1).astype(jnp.float32)
        score = jnp.where(spot < counts, score, NEG)
        top = jnp.max(score, axis=1, keepdims=True) * COEF
        acc = dot_nn(jnp.exp2(score * COEF - top).astype(jnp.bfloat16), value_x)
        total = acc[:, HD:]
        live = counts > 0.0
        part = jnp.where(live, acc[:, :HD] / total, 0.0).astype(jnp.bfloat16)
        stat = jnp.where(live, top * LN2 + jnp.log(total), NEG)
        return (
            [part[j * size : (j + 1) * size] for j in range(GROUP)],
            [stat[j * size : (j + 1) * size] for j in range(GROUP)],
        )

    step_rows = min(opts, 64)

    def options_blk():
        for base in range(0, opts, step_rows):
            span = pl.ds(base, step_rows)
            eye = lax.broadcasted_iota(jnp.int32, (step_rows, opts), 0) + base
            eye = eye == lax.broadcasted_iota(jnp.int32, (step_rows, opts), 1)
            col = jnp.sum(jnp.where(eye, length, 0.0), axis=1, keepdims=True)
            start = (me * rows).astype(jnp.float32)
            count = jnp.clip(col - start, 0.0, float(rows))
            lanes = lax.broadcasted_iota(jnp.int32, (step_rows, HD), 1)
            stats = jnp.zeros((step_rows, HD), jnp.float32)
            for g in range(kvs):
                queries = oq_ref[span, pl.ds(g * GROUP * HD, GROUP * HD)]
                parts, tops = opt_attend(queries, count, k_ref[:, pl.ds(g * HD, HD)], vx_ref[g])
                for j in range(GROUP):
                    h = g * GROUP + j
                    part_ref[span, pl.ds(h * HD, HD)] = parts[j]
                    stats = jnp.where(lanes == h, tops[j], stats)
            stat_ref[span, :] = stats
        slots = lax.broadcasted_iota(jnp.int32, (CAP, opts), 0)
        for d in range(n):
            hot = (slots + d * CAP == dest).astype(jnp.float32)
            span = pl.ds(d * CAP, CAP)
            pbuf[span, :] = dot_nn(hot.astype(jnp.bfloat16), part_ref[...]).astype(jnp.bfloat16)
            sbuf[span, :] = dot_nn(hot, stat_ref[...], lax.Precision.HIGHEST)

    def part_copies(step):
        to = lax.rem(me + step, n)
        span = pl.ds(pl.multiple_of(to * CAP, CAP), CAP)
        return (
            pltpu.make_async_remote_copy(
                src_ref=pbuf.at[span],
                dst_ref=rx_p.at[me],
                send_sem=p_send.at[step - 1],
                recv_sem=p_recv.at[step - 1],
                device_id={"blk": to},
                device_id_type=MESH,
            ),
            pltpu.make_async_remote_copy(
                src_ref=sbuf.at[span],
                dst_ref=rx_s.at[me],
                send_sem=s_send.at[step - 1],
                recv_sem=s_recv.at[step - 1],
                device_id={"blk": to},
                device_id_type=MESH,
            ),
        )

    mine_hot = (lax.broadcasted_iota(jnp.int32, (CAP, opts), 0) + me * CAP) == dest

    def options_anchor(key_of, value_of):
        count = jnp.sum(jnp.where(mine_hot, length, 0.0), axis=1, keepdims=True)
        count = jnp.clip(count, 0.0, float(rows))
        hot = mine_hot.astype(jnp.float32).astype(jnp.bfloat16)
        lanes = lax.broadcasted_iota(jnp.int32, (CAP, HD), 1)
        stats = jnp.zeros((CAP, HD), jnp.float32)
        for g in range(kvs):
            cols = pl.ds(g * GROUP * HD, GROUP * HD)
            queries = dot_nn(hot, oq_ref[:, cols]).astype(jnp.bfloat16)
            parts, tops = opt_attend(queries, count, key_of[:, pl.ds(g * HD, HD)], value_of[g])
            for j in range(GROUP):
                h = g * GROUP + j
                rx_p[0, :, pl.ds(h * HD, HD)] = parts[j]
                stats = jnp.where(lanes == h, tops[j], stats)
        rx_s[0] = stats

    for copy in q_copies:
        copy.wait()
    lax.fori_loop(0, cut, local_pair, 0)
    o_copy.wait()
    oq_up_arrived(n - 1)
    for step in range(1, n):
        @pl.when(me + step < n)
        def _():
            oq_down(step).wait_recv()

    @pl.when(me > 0)
    def _():
        options_blk()

    lax.fori_loop(cut, pairs, local_pair, 0)

    def send_parts(upward):
        for step in range(1, n):
            @pl.when((me + step < n) if upward else (me + step >= n))
            def _():
                for copy in part_copies(step):
                    copy.start()

    @pl.when(me > 0)
    def _():
        send_parts(False)
        for c in range(QUARTERS):
            @pl.when(c + offset >= pairs)
            def _():
                forward(c)

        own_slots = pl.ds(pl.multiple_of(me * CAP, CAP), CAP)
        rx_p[me] = pbuf[own_slots, :]
        rx_s[me] = sbuf[own_slots, :]

    def out_copy(i):
        cols = pl.ds(pl.multiple_of(i * PAIR * HD, PAIR * HD), PAIR * HD)
        return pltpu.make_async_copy(out_ref.at[:, cols], ctx_hbm.at[:, cols], out_sem.at[i])

    @pl.when(me == 0)
    def _():
        def finish(i, carry):
            for j in range(PAIR):
                h = i * PAIR + j
                out_ref[:, head_cols(h)] = (
                    acc_ref[h, :, pl.ds(0, HD)] / acc_ref[h, :, pl.ds(HD, HD)]
                ).astype(jnp.bfloat16)
            out_copy(i).start()
            return carry

        lax.fori_loop(0, pairs, finish, 0)
        options_anchor(k_ref, vx_ref)

    @pl.when(me > 0)
    def _():
        def finish(i, carry):
            anchor_heads([i * PAIR + j for j in range(PAIR)])
            out_copy(i).start()

            at = i + jnp.maximum(pairs - offset, QUARTERS)

            @pl.when(at < chunks)
            def _():
                forward(at)

            @pl.when(i == max(chunks - QUARTERS - 1, 0))
            def _():
                send_parts(True)

            return carry

        lax.fori_loop(0, pairs, finish, 0)
        options_anchor(ak_ref, avx_ref)

    for step in range(1, n):
        @pl.when(lax.rem(me - step + n, n) > 0)
        def _():
            for copy in part_copies(step):
                copy.wait_recv()

    top = rx_s[0]
    for b in range(1, n):
        top = jnp.maximum(top, rx_s[b])
    total = jnp.zeros_like(top)
    for b in range(n):
        total = total + jnp.exp(rx_s[b] - top)
    occupied = jnp.sum(mine_hot.astype(jnp.float32), axis=1, keepdims=True) > 0.0
    for h in range(heads):
        cols = pl.ds(h * HD, HD)
        merged = jnp.zeros((CAP, HD), jnp.float32)
        for b in range(n):
            weight = jnp.exp(rx_s[b, :, pl.ds(h, 1)] - top[:, h : h + 1])
            merged = merged + weight * rx_p[b, :, cols].astype(jnp.float32)
        merged = merged / total[:, h : h + 1]
        opt_ref[:, cols] = jnp.where(occupied, merged, 0.0).astype(jnp.bfloat16)

    for step in range(1, n):
        @pl.when(me >= step)
        def _():
            oq_down(step).wait_send()

        @pl.when((me >= step - 1) & (me < n - 1))
        def _():
            oq_up(step).wait_send()

    @pl.when(me == 0)
    def _():
        def drain(c, carry):
            for copy in anchor_copies(c, True):
                copy.wait_send()
            return carry

        lax.fori_loop(0, chunks, drain, 0)

    @pl.when((me > 0) & (me < n - 1))
    def _():
        def drain(c, carry):
            for copy in anchor_copies(c, False):
                copy.wait_send()
            return carry

        lax.fori_loop(0, chunks, drain, 0)

    @pl.when(me > 0)
    def _():
        for step in range(1, n):
            for copy in part_copies(step):
                copy.wait_send()

    def drain_out(i, carry):
        out_copy(i).wait()
        return carry

    lax.fori_loop(0, pairs, drain_out, 0)


def body(ctx_query, ctx_key, ctx_value, opt_query, opt_owner, opt_slot, opt_length):
    n = lax.axis_size("blk")
    rows, width = ctx_query.shape
    heads = width // HD
    kvs = ctx_key.shape[1] // HD
    opts = opt_length.shape[0]
    entry = opt_query.shape[0]
    chunks = QUARTERS * kvs
    bf16, f32 = jnp.bfloat16, jnp.float32
    dma = pltpu.SemaphoreType.DMA
    hbm = pl.BlockSpec(memory_space=pl.ANY)
    vmem = pl.BlockSpec(memory_space=pltpu.VMEM)
    return pl.pallas_call(
        functools.partial(kernel, n),
        out_shape=(
            jax.ShapeDtypeStruct((rows, width), bf16),
            jax.ShapeDtypeStruct((CAP, width), bf16),
        ),
        in_specs=[hbm, hbm, hbm, hbm, vmem, vmem, vmem],
        out_specs=(hbm, vmem),
        scratch_shapes=[
            pltpu.VMEM((rows, width), bf16),
            pltpu.VMEM((rows, kvs * HD), bf16),
            pltpu.VMEM((kvs, rows, 2 * HD), bf16),
            pltpu.VMEM((rows, kvs * HD), bf16),
            pltpu.VMEM((kvs, rows, 2 * HD), bf16),
            pltpu.VMEM((opts, width), bf16),
            pltpu.VMEM((heads, rows, 2 * HD), f32),
            pltpu.VMEM((heads, rows, HD), f32),
            pltpu.VMEM((rows, width), bf16),
            pltpu.VMEM((opts, width), bf16),
            pltpu.VMEM((opts, HD), f32),
            pltpu.VMEM((n * CAP, width), bf16),
            pltpu.VMEM((n * CAP, HD), f32),
            pltpu.VMEM((n, CAP, width), bf16),
            pltpu.VMEM((n, CAP, HD), f32),
            dma((2,)), dma(()), dma((kvs,)), dma(()), dma((heads // PAIR,)),
            dma((n - 1,)), dma((n - 1,)), dma((n - 1,)), dma((n - 1,)),
            dma((chunks,)), dma((chunks,)), dma((chunks,)), dma((chunks,)),
            dma((n - 1,)), dma((n - 1,)), dma((n - 1,)), dma((n - 1,)),
        ],
        compiler_params=pltpu.CompilerParams(
            collective_id=0, has_side_effects=True, vmem_limit_bytes=60 * 1024 * 1024
        ),
        name="star",
    )(ctx_query, ctx_key, ctx_value, opt_query, *(x.reshape(1, opts) for x in (opt_length, opt_owner, opt_slot)))


def solution(mesh):
    return jax.shard_map(
        body,
        mesh=mesh,
        in_specs=(
            P(("groups", "blk"), "head"),
            P(("groups", "blk"), "head"),
            P(("groups", "blk"), "head"),
            P(("groups", "blk"), "head"),
            P("groups"),
            P("groups"),
            P("groups"),
        ),
        out_specs=(P(("groups", "blk"), "head"), P(("groups", "blk"), "head")),
        check_vma=False,
    )
```
